32 devices in a mesh: snap: 8 (over z, core), vtx: 4 (over y, x).
Axes of the slice: x: 2, y: 2, z: 4, core: 2. Of those that a mesh axis runs over, the one named last changes fastest.
Arguments:
- feats: float32 [8, 4096, 512], P('snap', 'vtx'), may hold values from -6 to 6
- col_ids: int32 [8, 32, 16], P('snap', 'vtx'), may hold values from 0 to 31
- tiles: float32 [8, 32, 16, 128, 128], P('snap', 'vtx'), may hold values from -0.125 to 0.125
- w_first: float32 [512, 256], replicated, may hold values from -0.25 to 0.25
- w_input: float32 [256, 1024], replicated, may hold values from -0.375 to 0.375
- w_recur: float32 [256, 1024], replicated, may hold values from -0.375 to 0.375
- lstm_bias: float32 [1024], replicated, may hold values from -3 to 3
- w_second: float32 [256, 256], replicated, may hold values from -0.375 to 0.375
Outputs:
- output: float32 [8, 4096, 256], P('snap', 'vtx')
The draws below stay inside these ranges and needn't reach their ends.
Inputs may be any that keep to these rules, and one draw needn't show every extreme that they name: `col_ids`: every entry names a row block of the same snapshot's graph; a few blocks are named far more often than others.
All inputs are finite; a program needn't handle non-finite values.
Results may differ from the reference program's by a relative error of at most 0.0003.
Values sent between devices are 32-bit elements; how exact they have to be, the bound alone decides.
No kernel may reach another device: no remote copies, remote signals or barrier semaphores. Data moves between devices by JAX's collectives and lax.ppermute only.
A program may use at most 128 MiB of HBM per device.

```python
import math
import jax
import jax.numpy as jnp
import numpy as np
from jax import lax

F = 512
H = 256
TILE = 128
KT = 16
NBLK = 32
VERTS = 4096
SNAPS = 8


def set_ends(entries, stream_key, low, top_value):
    dims = entries.shape
    place = [jax.random.randint(jax.random.fold_in(stream_key, axis), (), 0, dims[axis]) for axis in range(len(dims))]
    entries = entries.at[tuple(place)].set(low)
    longest = dims.index(max(dims))
    place[longest] = (place[longest] + 1) % dims[longest]
    return entries.at[tuple(place)].set(top_value)


def block_scale(key, extent, pieces, least, top_value):
    level, own = 1.0, jax.random.fold_in(key, 6)
    for position, parts in pieces:
        heights = jnp.exp(jax.random.uniform(jax.random.fold_in(own, position), (parts,), jnp.float32, least / len(pieces), top_value / len(pieces)))
        level = level * jnp.repeat(heights, extent[position] // parts).reshape([-1 if axis == position else 1 for axis in range(len(extent))])
    return level


def cumulative_ranks(amount, lean):
    weights = [(1 << 20) // math.isqrt(rank ** lean) + 1 for rank in range(1, amount + 1)]
    scale = 1 + sum(weights) // (1 << 30)
    return np.cumsum(np.array([max(1, weight // scale) for weight in weights]))


def skewed_ids(stream_key, extent, number_of, slope):
    table = cumulative_ranks(number_of, slope)
    lot = jax.random.randint(jax.random.fold_in(stream_key, 1), extent, 0, int(table[number_of - 1]))
    standing = jnp.searchsorted(jnp.asarray(table, jnp.int32), lot, side="right")
    return jax.random.permutation(jax.random.fold_in(stream_key, 2), number_of)[standing].astype(jnp.int32)


def centred(own_key, dims, scale, limit, cuts=(), dtype=jnp.bfloat16):
    factor_of = block_scale(own_key, dims, cuts, -0.22, 0.18) if cuts else 1.0
    entries = jax.random.normal(own_key, dims, jnp.float32) * scale * factor_of
    return jnp.minimum(jnp.maximum(entries, -limit), limit).astype(dtype)


def setup_inputs(seed: int = 0) -> dict:
    keys = jax.random.split(jax.random.key(seed), 9)
    return {
        "feats": centred(keys[0], (SNAPS, VERTS, F), 1.0, 6.0, ((0, 8), (1, 4)), jnp.float32),
        "col_ids": set_ends(skewed_ids(keys[1], (SNAPS, NBLK, KT), NBLK, 2), jax.random.fold_in(keys[1], 3), 0, NBLK - 1).astype(jnp.int32),
        "tiles": centred(keys[2], (SNAPS, NBLK, KT, TILE, TILE), (KT * TILE) ** -0.5, 0.125, ((0, 8), (1, 4)), jnp.float32),
        "w_first": centred(keys[3], (F, H), F ** -0.5, 0.25, (), jnp.float32),
        "w_input": centred(keys[4], (H, 4 * H), H ** -0.5, 0.375, (), jnp.float32),
        "w_recur": centred(keys[5], (H, 4 * H), H ** -0.5, 0.375, (), jnp.float32),
        "lstm_bias": centred(keys[6], (4 * H,), 0.7, 3.0, (), jnp.float32),
        "w_second": centred(keys[7], (H, H), H ** -0.5, 0.375, (), jnp.float32),
    }


def block_sum(tile_set, column_ids, source):
    tile_edge = tile_set.shape[-1]
    width = source.shape[-1]
    blocks = source.reshape(source.shape[0] // tile_edge, tile_edge, width)

    def row_block(operands):
        tiles_here, ids_here = operands
        picked = blocks[ids_here.astype(jnp.int32)]
        return jnp.einsum('ktu,kuw->tw', tiles_here, picked, precision=lax.Precision.HIGHEST)
    summed = lax.map(row_block, (tile_set, column_ids))
    return summed.reshape(-1, width)

def row_scale(tiles):
    sums = lax.optimization_barrier(jnp.sum(tiles * tiles, axis=(2, 4)))
    return lax.rsqrt(1.0 + sums).reshape(tiles.shape[0], -1)[..., None]

def recurrence(pre_time, w_recur, lstm_bias):
    hidden_size = w_recur.shape[0]

    def advance(carry, pre_step):
        state_h, state_c = carry
        gates = pre_step + jnp.dot(state_h, w_recur, precision=lax.Precision.HIGHEST) + lstm_bias
        gate_i = gates[:, :hidden_size]
        gate_f = gates[:, hidden_size:2 * hidden_size]
        gate_g = gates[:, 2 * hidden_size:3 * hidden_size]
        gate_o = gates[:, 3 * hidden_size:]
        state_c = jax.nn.sigmoid(gate_f) * state_c + jax.nn.sigmoid(gate_i) * jnp.tanh(gate_g)
        state_h = jax.nn.sigmoid(gate_o) * jnp.tanh(state_c)
        return ((state_h, state_c), state_h)
    zeros = jnp.zeros((pre_time.shape[1], hidden_size), jnp.float32)
    _, states = lax.scan(advance, (zeros, zeros), pre_time)
    return states

def reference(feats, col_ids, tiles, w_first, w_input, w_recur, lstm_bias, w_second):
    scale = row_scale(tiles)
    mixed = scale * (feats + jax.vmap(block_sum)(tiles, col_ids, feats))
    hidden_one = jax.nn.relu(jnp.einsum('svf,fh->svh', mixed, w_first, precision=lax.Precision.HIGHEST))
    pre = jnp.einsum('svh,hg->svg', hidden_one, w_input, precision=lax.Precision.HIGHEST)
    states = recurrence(pre, w_recur, lstm_bias)
    mixed_two = scale * (states + jax.vmap(block_sum)(tiles, col_ids, states))
    return jnp.einsum('svh,hg->svg', mixed_two, w_second, precision=lax.Precision.HIGHEST)
```

```python
import functools

import jax
import jax.numpy as jnp
from jax import lax
from jax.experimental import pallas as pl
from jax.experimental.pallas import tpu as pltpu
from jax.sharding import PartitionSpec as P

F32 = jnp.float32
BF16 = jnp.bfloat16
VMEM = pltpu.VMEM


def split(x):
    high = x.astype(BF16)
    return high, (x - high.astype(F32)).astype(BF16)


def mm(a, b):
    return jnp.dot(a, b, preferred_element_type=F32)


def params(mib):
    return pltpu.CompilerParams(vmem_limit_bytes=mib << 20)


def cost(flops, moved):
    return pl.CostEstimate(flops=int(flops), bytes_accessed=int(moved), transcendentals=0)


def whole():
    return pl.BlockSpec(memory_space=VMEM)


def project_kernel(x_ref, w_ref, *rest):
    outs, (wh, wl) = rest[:-2], rest[-2:]

    @pl.when(pl.program_id(0) == 0)
    def _():
        wh[...], wl[...] = split(w_ref[...])

    xh, xl = split(x_ref[...])
    y = mm(xh, wh[...]) + mm(xl, wh[...]) + mm(xh, wl[...])
    n = outs[0].shape[1]
    for q, out in enumerate(outs):
        out[...] = y[:, q * n : (q + 1) * n]


def project(x, w, chunks):
    rows, depth = x.shape
    width = w.shape[1]
    n = width // chunks
    block = min(rows, 256)
    return pl.pallas_call(
        project_kernel,
        grid=(rows // block,),
        in_specs=[pl.BlockSpec((block, depth), lambda i: (i, 0)), pl.BlockSpec((depth, width), lambda i: (0, 0))],
        out_specs=[pl.BlockSpec((block, n), lambda i: (i, 0))] * chunks,
        out_shape=[jax.ShapeDtypeStruct((rows, n), F32)] * chunks,
        scratch_shapes=[VMEM((depth, width), BF16)] * 2,
        compiler_params=params(16),
        cost_estimate=cost(6 * rows * depth * width, 4 * rows * (depth + width)),
        name="project",
    )(x, w)


def prepare_kernel(t_ref, a_ref, s_ref):
    _, kt, tile, _ = t_ref.shape
    total = jnp.zeros((tile, tile), F32)
    for k in range(kt):
        t = t_ref[0, k]
        total = total + t * t
        high, low = split(t)
        a_ref[0, :tile, k * tile : (k + 1) * tile] = high
        a_ref[0, tile:, k * tile : (k + 1) * tile] = low
    s = lax.rsqrt(1.0 + jnp.sum(total, axis=1, keepdims=True))
    s_ref[0] = jnp.broadcast_to(s, (tile, tile))


def prepare(tiles):
    nb, kt, tile, _ = tiles.shape
    return pl.pallas_call(
        prepare_kernel,
        grid=(nb,),
        in_specs=[pl.BlockSpec((1, kt, tile, tile), lambda i: (i, 0, 0, 0))],
        out_specs=[
            pl.BlockSpec((1, 2 * tile, kt * tile), lambda i: (i, 0, 0)),
            pl.BlockSpec((1, tile, tile), lambda i: (i, 0, 0)),
        ],
        out_shape=[
            jax.ShapeDtypeStruct((nb, 2 * tile, kt * tile), BF16),
            jax.ShapeDtypeStruct((nb, tile, tile), F32),
        ],
        compiler_params=params(16),
        cost_estimate=cost(8 * tiles.size, 8 * tiles.size),
        name="prepare",
    )(tiles)


def weights_kernel(*refs):
    n = len(refs) // 3
    for i in range(n):
        refs[n + 2 * i][...], refs[n + 2 * i + 1][...] = split(refs[i][...])


def split_weights(*ws):
    shapes = [jax.ShapeDtypeStruct(w.shape, BF16) for w in ws for _ in range(2)]
    return pl.pallas_call(
        weights_kernel,
        in_specs=[whole()] * len(ws),
        out_specs=[whole()] * len(shapes),
        out_shape=shapes,
        compiler_params=params(16),
        cost_estimate=cost(1, 8 * sum(w.size for w in ws)),
        name="split_weights",
    )(*ws)


def conv_one_kernel(shape, cols, place, a_ref, s_ref, own_ref, *rest):
    n_parts, chips, sub_rows = shape
    parts, outs, y, hold = rest[:n_parts], rest[n_parts:-2], rest[-2], rest[-1]
    r = pl.program_id(0)
    tile = s_ref.shape[1]
    n = own_ref.shape[1]
    snap, slab = place[0], place[1]

    @pl.when(r == 0)
    def _():
        rows = own_ref.shape[0]
        fill(y, [own_ref], slab * rows)
        if n_parts == 4:
            fill(y, [parts[0]], (slab ^ 1) * rows)
            fill(y, [parts[1]], (slab ^ 2) * rows)
            fill(y, parts[2:], (slab ^ 3) * rows)
        else:
            fill(y, [parts[0]], 0)

    acc = None
    kt = cols.shape[1]
    for p in range(0, kt, 2):
        rhs = jnp.concatenate([y[pl.ds(pl.multiple_of(cols[r, p + i] * tile, tile), tile), :] for i in range(2)], axis=0)
        term = mm(a_ref[0, :, p * tile : (p + 2) * tile], rhs)
        acc = term if acc is None else acc + term
    own = own_ref[pl.ds(pl.multiple_of(r * tile, tile), tile), :]
    mixed = own + acc[:tile, :n] + acc[:tile, n:] + acc[tile:, :n]
    hidden = jnp.maximum(s_ref[0][:, :n] * mixed, 0.0)
    for i in range(tile // sub_rows):
        j = r * (tile // sub_rows) + i
        hold[j ^ snap] = hidden[i * sub_rows : (i + 1) * sub_rows]

    @pl.when(r == pl.num_programs(0) - 1)
    def _():
        for i, out in enumerate(outs):
            out[...] = hold[i]


def fill(y, refs, start):
    at = 0
    n = y.shape[1] // 2
    for ref in refs:
        for b in range(0, ref.shape[0], 128):
            high, low = split(ref[b : b + 128])
            where = pl.ds(pl.multiple_of(start + at + b, 128), 128)
            y[where, :n] = high
            y[where, n:] = low
        at += ref.shape[0]


def conv_one(cols, place, a, s, own, parts, n_snap):
    nb, two, deep = a.shape
    tile = two // 2
    rows, n = own.shape
    verts = rows * (len(parts) if len(parts) == 4 else 1)
    if len(parts) != 4:
        verts = parts[0].shape[0]
    sub = rows // n_snap
    shape = (len(parts), n_snap // 2, sub)
    grid_spec = pltpu.PrefetchScalarGridSpec(
        num_scalar_prefetch=2,
        grid=(nb,),
        in_specs=[
            pl.BlockSpec((1, two, deep), lambda i, *_: (i, 0, 0)),
            pl.BlockSpec((1, tile, tile), lambda i, *_: (i, 0, 0)),
        ]
        + [whole()] * (1 + len(parts)),
        out_specs=[whole()] * n_snap,
        scratch_shapes=[VMEM((verts, 2 * n), BF16), VMEM((n_snap, sub, n), F32)],
    )
    return pl.pallas_call(
        functools.partial(conv_one_kernel, shape),
        grid_spec=grid_spec,
        out_shape=[jax.ShapeDtypeStruct((sub, n), F32)] * n_snap,
        compiler_params=params(32),
        cost_estimate=cost(2 * nb * two * deep * 2 * n, 2 * a.size + 4 * verts * n),
        name="conv_one",
    )(cols, place, a, s, own, *parts)


def sigmoid(x):
    return 0.5 * jnp.tanh(0.5 * x) + 0.5


def lstm_kernel(n_snap, chunks, place, *refs):
    pieces = refs[: n_snap * chunks]
    wih, wil, wrh, wrl, bias = refs[n_snap * chunks : n_snap * chunks + 5]
    outs = refs[n_snap * chunks + 5 : -3]
    xh, xl, pre = refs[-3:]
    snap = place[0]
    sub, n = pieces[0].shape
    width = n * chunks
    for q in range(chunks):
        for i in range(n_snap):
            high, low = split(pieces[q * n_snap + i][...])
            where = pl.ds(pl.multiple_of((snap ^ i) * sub, sub), sub)
            xh[where, q * n : (q + 1) * n] = high
            xl[where, q * n : (q + 1) * n] = low
    pre[...] = mm(xh[...], wih[...]) + mm(xl[...], wih[...]) + mm(xh[...], wil[...]) + bias[...]
    h = c = None
    for s in range(n_snap):
        gates = pre[s * sub : (s + 1) * sub]
        if s:
            high, low = split(h)
            both = mm(jnp.concatenate([high, low], axis=0), wrh[...])
            gates = gates + both[:sub] + both[sub:] + mm(high, wrl[...])
        gi, gf, gg, go = (gates[:, i * width : (i + 1) * width] for i in range(4))
        new = sigmoid(gi) * jnp.tanh(gg)
        c = new if c is None else sigmoid(gf) * c + new
        h = sigmoid(go) * jnp.tanh(c)
        pre[pl.ds(pl.multiple_of((s ^ snap) * 0 + s * sub, sub), sub), :width] = h
    for i, out in enumerate(outs):
        out[...] = pre[pl.ds(pl.multiple_of((i ^ snap) * sub, sub), sub), :width]


def lstm(place, pieces, weights, bias, n_snap, chunks):
    sub, n = pieces[0].shape
    width = n * chunks
    smem = pl.BlockSpec(memory_space=pltpu.SMEM)
    return pl.pallas_call(
        functools.partial(lstm_kernel, n_snap, chunks),
        in_specs=[smem] + [whole()] * (len(pieces) + 5),
        out_specs=[whole()] * n_snap,
        out_shape=[jax.ShapeDtypeStruct((sub, width), F32)] * n_snap,
        scratch_shapes=[VMEM((n_snap * sub, width), BF16)] * 2 + [VMEM((n_snap * sub, 4 * width), F32)],
        compiler_params=params(32),
        cost_estimate=cost(12 * n_snap * sub * width * 4 * width, 8 * n_snap * sub * width),
        name="lstm",
    )(place, *pieces, *weights, bias)


def conv_two_kernel(plan, cols, place, a_ref, s_ref, w_ref, *rest):
    groups, n_parts = plan
    n_in = len(groups) * (1 + n_parts)
    ins, out_ref, yh, yl, own, wh, wl = rest[:n_in], rest[n_in], *rest[n_in + 1 :]
    r = pl.program_id(0)
    tile = s_ref.shape[1]
    rows = own.shape[0]
    snap, slab = place[0], place[1]

    def put(ref, i, j, v, keep):
        value = ref[i]
        sub = value.shape[0]
        high, low = split(value)
        where = pl.ds(pl.multiple_of(v * rows + j * sub, sub), sub)
        yh[where, :] = high
        yl[where, :] = low
        if keep:
            own[pl.ds(pl.multiple_of(j * sub, sub), sub), :] = value

    @pl.when(r == 0)
    def _():
        wh[...], wl[...] = split(w_ref[...])
        for g, members in enumerate(groups):
            refs = ins[g * (1 + n_parts) : (g + 1) * (1 + n_parts)]
            half = len(members) // 2
            for i, m in enumerate(members):
                j = m ^ snap
                put(refs[0], i, j, slab, True)
                if n_parts == 4:
                    put(refs[1], i, j, slab ^ 1, False)
                    put(refs[2], i, j, slab ^ 2, False)
                    put(refs[3 if i < half else 4], i % half, j, slab ^ 3, False)
                else:
                    for v in range(refs[1].shape[0]):
                        put(refs[1].at[v], i, j, v, False)

    one = two = None
    kt = cols.shape[1]
    for p in range(0, kt, 2):
        at = [pl.ds(pl.multiple_of(cols[r, p + i] * tile, tile), tile) for i in range(2)]
        high = jnp.concatenate([yh[w, :] for w in at], axis=0)
        low = jnp.concatenate([yl[w, :] for w in at], axis=0)
        t1 = mm(a_ref[0, :, p * tile : (p + 2) * tile], high)
        t2 = mm(a_ref[0, :tile, p * tile : (p + 2) * tile], low)
        one = t1 if one is None else one + t1
        two = t2 if two is None else two + t2
    mine = own[pl.ds(pl.multiple_of(r * tile, tile), tile), :]
    mixed = s_ref[0][:, :1] * (mine + one[:tile] + one[tile:] + two)
    mh, ml = split(mixed)
    out_ref[...] = mm(mh, wh[...]) + mm(ml, wh[...]) + mm(mh, wl[...])


def conv_two(cols, place, a, s, w, groups, ins, n_parts, verts, rows):
    nb, two, deep = a.shape
    tile = two // 2
    width = w.shape[0]
    grid_spec = pltpu.PrefetchScalarGridSpec(
        num_scalar_prefetch=2,
        grid=(nb,),
        in_specs=[
            pl.BlockSpec((1, two, deep), lambda i, *_: (i, 0, 0)),
            pl.BlockSpec((1, tile, tile), lambda i, *_: (i, 0, 0)),
        ]
        + [whole()] * (1 + len(ins)),
        out_specs=pl.BlockSpec((tile, w.shape[1]), lambda i, *_: (i, 0)),
        scratch_shapes=[VMEM((verts, width), BF16)] * 2 + [VMEM((rows, width), F32)] + [VMEM(w.shape, BF16)] * 2,
    )
    return pl.pallas_call(
        functools.partial(conv_two_kernel, (groups, n_parts)),
        grid_spec=grid_spec,
        out_shape=jax.ShapeDtypeStruct((rows, w.shape[1]), F32),
        compiler_params=params(40),
        cost_estimate=cost(3 * nb * two * deep * width, 2 * a.size + 4 * verts * width),
        name="conv_two",
    )(cols, place, a, s, w, *ins)


def gather(x, n_vtx):
    if n_vtx != 4:
        return [lax.all_gather(x, "vtx", axis=0)]
    flip = lambda bit: [(i, i ^ bit) for i in range(n_vtx)]
    from_x = lax.ppermute(x, "vtx", flip(1))
    from_y = lax.ppermute(x, "vtx", flip(2))
    half = x.shape[0] // 2
    first = lax.ppermute(from_y[:half], "vtx", flip(1))
    second = lax.ppermute(from_x[half:], "vtx", flip(2))
    return [from_x, from_y, first, second]


def exchange(pieces, n_snap):
    flip = lambda bits: [(i, i ^ bits) for i in range(n_snap)]
    return [p if i == 0 else lax.ppermute(p, "snap", flip(i)) for i, p in enumerate(pieces)]


def on_device(n_snap, n_vtx, feats, col_ids, tiles, w_first, w_input, w_recur, lstm_bias, w_second):
    chunks = 2
    x, cols = feats[0], col_ids[0]
    rows = x.shape[0]
    verts = rows * n_vtx
    place = jnp.stack([lax.axis_index("snap"), lax.axis_index("vtx")]).astype(jnp.int32)
    projected = project(x, w_first, chunks)
    gathered = [gather(p, n_vtx) for p in projected]
    a, s = prepare(tiles[0])
    weights = split_weights(w_input, w_recur)
    pieces = []
    for own, parts in zip(projected, gathered):
        if n_vtx != 4:
            parts = [parts[0].reshape(verts, own.shape[1])]
        pieces += exchange(conv_one(cols, place, a, s, own, parts, n_snap), n_snap)
    states = lstm(place, pieces, weights, lstm_bias[None], n_snap, chunks)
    back = exchange(states, n_snap)
    groups = [tuple(range(n_snap // 2)), tuple(range(n_snap // 2, n_snap))]
    ins = []
    for members in groups:
        block = jnp.stack([back[m] for m in members])
        ins += [block] + gather(block, n_vtx)
    n_parts = 4 if n_vtx == 4 else 1
    out = conv_two(cols, place, a, s, w_second, groups, ins, n_parts, verts, rows)
    return out[None]


def solution(mesh):
    placed = (
        P("snap", "vtx", None),
        P("snap", "vtx", None),
        P("snap", "vtx", None, None, None),
        P(),
        P(),
        P(),
        P(),
        P(),
    )
    body = functools.partial(on_device, mesh.shape["snap"], mesh.shape["vtx"])
    return jax.shard_map(body, mesh=mesh, in_specs=placed, out_specs=P("snap", "vtx", None), check_vma=False)
```

```python
import functools

import jax
import jax.numpy as jnp
from jax import lax
from jax.experimental import pallas as pl
from jax.experimental.pallas import tpu as pltpu
from jax.sharding import PartitionSpec as P


F32 = jnp.float32
BF16 = jnp.bfloat16
VMEM = pltpu.VMEM


def split(x):
    high = x.astype(BF16)
    return high, (x - high.astype(F32)).astype(BF16)


def mm(a, b):
    return jnp.dot(a, b, preferred_element_type=F32)


def params(mib):
    return pltpu.CompilerParams(vmem_limit_bytes=mib << 20)


def cost(flops, moved):
    return pl.CostEstimate(flops=int(flops), bytes_accessed=int(moved), transcendentals=0)


def whole():
    return pl.BlockSpec(memory_space=VMEM)


def project_kernel(x_ref, w_ref, *outs):
    wh, wl = split(w_ref[...])
    n = outs[0].shape[1]
    rows = outs[0].shape[0]
    block = min(rows, 256)
    for t in range(2):
        for b in range(0, rows, block):
            xh, xl = split(x_ref[t * rows + b : t * rows + b + block])
            y = mm(xh, wh) + mm(xl, wh) + mm(xh, wl)
            for q in range(len(outs) // 2):
                outs[2 * q + t][b : b + block] = y[:, q * n : (q + 1) * n]


def project(x, w, chunks):
    rows, depth = x.shape
    width = w.shape[1]
    n = width // chunks
    outs = pl.pallas_call(
        project_kernel,
        in_specs=[whole()] * 2,
        out_specs=[whole()] * (2 * chunks),
        out_shape=[jax.ShapeDtypeStruct((rows // 2, n), F32)] * (2 * chunks),
        compiler_params=params(12),
        cost_estimate=cost(6 * rows * depth * width, 4 * rows * (depth + width)),
        name="project",
    )(x, w)
    return [outs[2 * q : 2 * q + 2] for q in range(chunks)]


def prepare_kernel(t_ref, a_ref, s_ref):
    _, kt, tile, _ = t_ref.shape
    total = jnp.zeros((tile, tile), F32)
    for k in range(kt):
        t = t_ref[0, k]
        total = total + t * t
        high, low = split(t)
        a_ref[0, :tile, k * tile : (k + 1) * tile] = high
        a_ref[0, tile:, k * tile : (k + 1) * tile] = low
    s = lax.rsqrt(1.0 + jnp.sum(total, axis=1, keepdims=True))
    s_ref[0] = jnp.broadcast_to(s, (tile, tile))


def prepare(tiles):
    nb, kt, tile, _ = tiles.shape
    return pl.pallas_call(
        prepare_kernel,
        grid=(nb,),
        in_specs=[pl.BlockSpec((1, kt, tile, tile), lambda i: (i, 0, 0, 0))],
        out_specs=[
            pl.BlockSpec((1, 2 * tile, kt * tile), lambda i: (i, 0, 0)),
            pl.BlockSpec((1, tile, tile), lambda i: (i, 0, 0)),
        ],
        out_shape=[
            jax.ShapeDtypeStruct((nb, 2 * tile, kt * tile), BF16),
            jax.ShapeDtypeStruct((nb, tile, tile), F32),
        ],
        compiler_params=params(12),
        cost_estimate=cost(8 * tiles.size, 8 * tiles.size),
        name="prepare",
    )(tiles)


def weights_kernel(wi_ref, wr_ref, wo_ref, wih, wil, weh, wel):
    wih[...], wil[...] = split(wi_ref[...])
    n = wr_ref.shape[1]
    weh[:, :n], wel[:, :n] = split(wr_ref[...])
    weh[:, n:], wel[:, n:] = split(wo_ref[...])


def split_weights(w_input, w_recur, w_second):
    wide = (w_recur.shape[0], w_recur.shape[1] + w_second.shape[1])
    return pl.pallas_call(
        weights_kernel,
        in_specs=[whole()] * 3,
        out_specs=[whole()] * 4,
        out_shape=[jax.ShapeDtypeStruct(shape, BF16) for shape in (w_input.shape, w_input.shape, wide, wide)],
        compiler_params=params(12),
        cost_estimate=cost(1, 16 * w_input.size),
        name="split_weights",
    )(w_input, w_recur, w_second)


def place_of(source, slab):
    flipped, number, _ = source
    return slab ^ number if flipped else number


def conv_one_kernel(sources, sub, blocks, cols, a_ref, s_ref, *rest):
    if sources is None:
        y, own, outs, hold = rest[0], rest[1], rest[2:-1], rest[-1]
    else:
        refs, outs, y, own, hold = rest[: len(sources)], rest[len(sources) : -3], *rest[-3:]
    _, tile, _ = s_ref.shape
    rows, n = own.shape
    snap, slab = lax.axis_index("snap"), lax.axis_index("vtx")
    per = tile // sub
    for source, ref in zip(sources or (), refs if sources else ()):
        start = place_of(source, slab) * rows + source[2]
        for b in range(0, ref.shape[0], tile):
            value = ref[b : b + tile]
            where = pl.ds(pl.multiple_of(start + b, tile), tile)
            y[where, :n], y[where, n:] = split(value)
            if source[:2] == (True, 0):
                own[source[2] + b : source[2] + b + tile] = value

    @pl.loop(*blocks)
    def _(q):
        r = q ^ (snap // per)
        kt = cols.shape[1]
        rhs = jnp.concatenate([y[pl.ds(pl.multiple_of(cols[r, k] * tile, tile), tile), :] for k in range(kt)], axis=0)
        acc = mm(a_ref[r, :tile, :], rhs)
        low = mm(a_ref[r, tile:, :], rhs[:, :n])
        mine = own[pl.ds(pl.multiple_of(r * tile, tile), tile), :]
        hidden = jnp.maximum(s_ref[r][:, :n] * (mine + acc[:, :n] + acc[:, n:] + low), 0.0)
        for i in range(per):
            hold[(r * per + i) ^ snap] = hidden[i * sub : (i + 1) * sub]

    for i, out in enumerate(outs):
        out[...] = hold[blocks[0] * per + i]


def conv_one(cols, a, s, sources, arrays, n_snap, rows, verts, blocks, keep=False):
    nb, two, deep = a.shape
    n = arrays[1].shape[-1]
    sub = rows // n_snap
    per = two // 2 // sub
    count = (blocks[1] - blocks[0]) * per
    smem = pl.BlockSpec(memory_space=pltpu.SMEM)
    hold = VMEM((n_snap, sub, n), F32)
    outs = [jax.ShapeDtypeStruct((sub, n), F32)] * count
    held = [jax.ShapeDtypeStruct((verts, 2 * n), BF16), jax.ShapeDtypeStruct((rows, n), F32)]
    scratch = [hold]
    if keep:
        outs = outs + held
    elif sources is not None:
        scratch = [VMEM(h.shape, h.dtype) for h in held] + scratch
    return pl.pallas_call(
        functools.partial(conv_one_kernel, sources and tuple(sources), sub, blocks),
        in_specs=[smem] + [whole()] * (2 + len(arrays)),
        out_specs=[whole()] * len(outs),
        scratch_shapes=scratch,
        out_shape=outs,
        compiler_params=params(20),
        cost_estimate=cost(2 * nb * two * deep * 2 * n, 2 * a.size + 4 * verts * n),
        name="conv_one",
    )(cols, a, s, *arrays)


def sigmoid(x):
    return 0.5 * jnp.tanh(0.5 * x) + 0.5


def lstm_kernel(n_snap, chunks, *refs):
    pieces = refs[: n_snap * chunks]
    wih, wil, weh, wel, bias = refs[n_snap * chunks : n_snap * chunks + 5]
    outs = refs[n_snap * chunks + 5 : -3]
    xh, xl, done = refs[-3:]
    snap = lax.axis_index("snap")
    sub, n = pieces[0].shape
    width = n * chunks
    wide = 4 * width
    for q in range(chunks):
        for i in range(n_snap):
            high, low = split(pieces[q * n_snap + i][...])
            where = pl.ds(pl.multiple_of((snap ^ i) * sub, sub), sub)
            xh[where, q * n : (q + 1) * n] = high
            xl[where, q * n : (q + 1) * n] = low

    def fresh(s):
        at = slice(s * sub, (s + 1) * sub)
        both = mm(jnp.concatenate([xh[at], xl[at]], axis=0), wih[...])
        return both[:sub] + both[sub:] + mm(xh[at], wil[...]) + bias[...]

    c = recur = None
    following = fresh(0)
    for s in range(n_snap):
        at = slice(s * sub, (s + 1) * sub)
        gates = following if recur is None else following + recur
        following = fresh(s + 1) if s < n_snap - 1 else None
        gi, gf, gg, go = (gates[:, i * width : (i + 1) * width] for i in range(4))
        new = sigmoid(gi) * jnp.tanh(gg)
        c = new if c is None else sigmoid(gf) * c + new
        high, low = split(sigmoid(go) * jnp.tanh(c))
        first = 0 if s < n_snap - 1 else wide
        both = mm(jnp.concatenate([high, low], axis=0), weh[:, first:])
        both = both[:sub] + both[sub:] + mm(high, wel[:, first:])
        recur = both[:, :wide]
        done[at] = both[:, wide - first :]
    for i, out in enumerate(outs):
        out[...] = done[pl.ds(pl.multiple_of((i ^ snap) * sub, sub), sub), :]


def lstm(pieces, weights, bias, n_snap, chunks):
    sub, n = pieces[0].shape
    width = n * chunks
    return pl.pallas_call(
        functools.partial(lstm_kernel, n_snap, chunks),
        in_specs=[whole()] * (len(pieces) + 5),
        out_specs=[whole()] * n_snap,
        out_shape=[jax.ShapeDtypeStruct((sub, width), F32)] * n_snap,
        scratch_shapes=[VMEM((n_snap * sub, width), BF16)] * 2 + [VMEM((n_snap * sub, width), F32)],
        compiler_params=params(20),
        cost_estimate=cost(12 * n_snap * sub * width * 4 * width, 8 * n_snap * sub * width),
        name="lstm",
    )(*pieces, *weights, bias)


def conv_two_kernel(sources, cols, a_ref, s_ref, *rest):
    refs, out_ref, (yh, yl, own, ready, sems) = rest[: len(sources)], rest[len(sources)], rest[len(sources) + 1 :]
    nb, tile, _ = s_ref.shape
    rows = own.shape[0]
    snap, slab = lax.axis_index("snap"), lax.axis_index("vtx")
    for source, ref in zip(sources, refs):
        sub = ref.shape[0]
        at = (source[2] ^ snap) * sub
        where = pl.ds(pl.multiple_of(place_of(source, slab) * rows + at, sub), sub)
        value = ref[...]
        yh[where, :], yl[where, :] = split(value)
        if source[:2] == (True, 0):
            own[pl.ds(pl.multiple_of(at, sub), sub), :] = value

    def leave(r):
        where = pl.ds(pl.multiple_of(r * tile, tile), tile)
        return pltpu.make_async_copy(ready.at[where, :], out_ref.at[where, :], sems.at[r])

    @pl.loop(0, nb)
    def _(r):
        kt = cols.shape[1]
        at = [pl.ds(pl.multiple_of(cols[r, k] * tile, tile), tile) for k in range(kt)]
        high = jnp.concatenate([yh[w, :] for w in at], axis=0)
        low = jnp.concatenate([yl[w, :] for w in at], axis=0)
        ah, al = a_ref[r, :tile, :], a_ref[r, tile:, :]
        where = pl.ds(pl.multiple_of(r * tile, tile), tile)
        ready[where, :] = s_ref[r][:, :1] * (own[where, :] + (mm(ah, high) + mm(al, high) + mm(ah, low)))
        leave(r).start()

    for r in range(nb):
        leave(r).wait()


def conv_two(cols, a, s, sources, arrays, rows, verts):
    nb, two, deep = a.shape
    width = arrays[0].shape[-1]
    smem = pl.BlockSpec(memory_space=pltpu.SMEM)
    return pl.pallas_call(
        functools.partial(conv_two_kernel, tuple(sources)),
        in_specs=[smem] + [whole()] * (2 + len(arrays)),
        out_specs=pl.BlockSpec(memory_space=pltpu.HBM),
        scratch_shapes=[VMEM((verts, width), BF16)] * 2
        + [VMEM((rows, width), F32)] * 2
        + [pltpu.SemaphoreType.DMA((nb,))],
        out_shape=jax.ShapeDtypeStruct((rows, width), F32),
        compiler_params=params(24),
        cost_estimate=cost(3 * nb * two * deep * width, 2 * a.size + 4 * verts * width),
        name="conv_two",
    )(cols, a, s, *arrays)


def hop(x, axis, bits, size):
    return lax.ppermute(x, axis, [(i, i ^ bits) for i in range(size)])


def gather(x, n_vtx, at, by_x):
    if n_vtx != 4:
        every = lax.all_gather(x, "vtx", axis=0)
        return [(True, 0, at)] + [(False, v, at) for v in range(n_vtx)], [x] + [every[v] for v in range(n_vtx)]
    from_x = hop(x, "vtx", 1, n_vtx)
    from_y = hop(x, "vtx", 2, n_vtx)
    cross = hop(from_y, "vtx", 1, n_vtx) if by_x else hop(from_x, "vtx", 2, n_vtx)
    return [(True, m, at) for m in range(4)], [x, from_x, from_y, cross]


def exchange(pieces, n_snap):
    return [p if i == 0 else hop(p, "snap", i, n_snap) for i, p in enumerate(pieces)]


def on_device(n_snap, n_vtx, feats, col_ids, tiles, w_first, w_input, w_recur, lstm_bias, w_second):
    x, cols = feats[0], col_ids[0]
    rows = x.shape[0]
    verts = rows * n_vtx
    half = rows // 2
    nb = cols.shape[0]
    projected = project(x, w_first, 2)
    a, s = prepare(tiles[0])
    weights = split_weights(w_input, w_recur, w_second)
    pieces = []
    for name, own in zip("ab", projected):
        sources, arrays = [], []
        for t in range(2):
            more = gather(own[t], n_vtx, t * half, t == 1)
            sources += more[0]
            arrays += more[1]
        near, far = (0, nb // 2), (nb // 2, nb)
        if name == "a":
            hidden = conv_one(cols, a, s, sources, arrays, n_snap, rows, verts, (0, nb))
        else:
            *distant, y, kept = conv_one(cols, a, s, sources, arrays, n_snap, rows, verts, far, True)
        if name == "b":
            hidden = [*conv_one(cols, a, s, None, [y, kept], n_snap, rows, verts, near), *distant]
        pieces += exchange(hidden, n_snap)
    states = lstm(pieces, weights, lstm_bias[None], n_snap, 2)
    sources, arrays = [], []
    for i, piece in enumerate(exchange(states, n_snap)):
        more = gather(piece, n_vtx, i, i % 2 == 1)
        sources += more[0]
        arrays += more[1]
    out = conv_two(cols, a, s, sources, arrays, rows, verts)
    return out[None]


def solution(mesh):
    placed = (
        P("snap", "vtx", None),
        P("snap", "vtx", None),
        P("snap", "vtx", None, None, None),
        P(),
        P(),
        P(),
        P(),
        P(),
    )
    n_snap, n_vtx = mesh.shape["snap"], mesh.shape["vtx"]
    body = functools.partial(on_device, n_snap, n_vtx)
    return jax.shard_map(body, mesh=mesh, in_specs=placed, out_specs=P("snap", "vtx", None), check_vma=False)
```
